256 devices in a mesh: seq: 4 (over x_hi, core), tok: 64 (over y, z, x_lo).
Axes of the slice: x: 4 (x_hi: 2, x_lo: 2; x = x_hi * 2 + x_lo), y: 4, z: 8, core: 2. Of those that a mesh axis runs over, the one named last changes fastest.
Arguments:
- query_gate: float32 [4, 32768, 128], P('seq', 'tok'), may hold values from -6 to 6
- key_gate: float32 [4, 32768, 128], P('seq', 'tok'), may hold values from -6 to 6
- value_input: float32 [4, 32768, 128], P('seq', 'tok'), may hold values from -6 to 6
- out_grad: float32 [4, 32768, 128], P('seq', 'tok'), may hold values from -6 to 6
- filter_param: float32 [128, 32768], P('tok', 'seq'), may hold values from -6 to 6
Outputs:
- query_grad: float32 [4, 32768, 128], P('seq', 'tok')
- key_grad: float32 [4, 32768, 128], P('seq', 'tok')
- value_grad: float32 [4, 32768, 128], P('seq', 'tok')
- filter_grad: float32 [128, 32768], P('tok', 'seq')
The draws below stay inside these ranges and needn't reach their ends.
All inputs are finite; a program needn't handle non-finite values.
Results may differ from the reference program's by a relative error of at most 0.00014.
Values sent between devices are 32-bit elements; how exact they have to be, the bound alone decides.
No kernel may reach another device: no remote copies, remote signals or barrier semaphores. Data moves between devices by JAX's collectives and lax.ppermute only.
A program may use at most 128 MiB of HBM per device.

```python
import jax
import jax.numpy as jnp

C = 128
L = 32768
SEQS = 4


def level_of(rng, shape, shards, smallest, high):
    def one(dim, blocks):
        heights = jax.random.uniform(jax.random.fold_in(jax.random.fold_in(rng, 6), dim), (blocks,), jnp.float32, smallest / len(shards), high / len(shards))
        return jnp.repeat(jnp.exp(heights), shape[dim] // blocks).reshape((-1,) + (1,) * (len(shape) - dim - 1))

    level = one(*shards[0])
    for cut in shards[1:]:
        level = level * one(*cut)
    return level


def scatter_about(own_key, shape, spread, most, cuts=(), kind=jnp.bfloat16):
    result = spread * jax.random.normal(own_key, shape, jnp.float32)
    if cuts:
        result = result * level_of(own_key, shape, cuts, -0.22, 0.18)
    return jnp.clip(result, -most, most).astype(kind)


def setup_inputs(seed: int = 0) -> dict:
    streams_of = jax.random.split(jax.random.key(seed), 6)
    query_gate = scatter_about(streams_of[0], (SEQS, L, C), 1.0, 6.0, ((0, 4), (1, 64)), jnp.float32)
    key_gate = scatter_about(streams_of[1], (SEQS, L, C), 1.0, 6.0, ((0, 4), (1, 64)), jnp.float32)
    value_input = scatter_about(streams_of[2], (SEQS, L, C), 1.0, 6.0, ((0, 4), (1, 64)), jnp.float32)
    out_grad = scatter_about(streams_of[3], (SEQS, L, C), 1.0, 6.0, ((0, 4), (1, 64)), jnp.float32)
    filter_param = scatter_about(streams_of[4], (C, L), 1.0, 6.0, ((0, 64), (1, 4)), jnp.float32)
    return dict(query_gate=query_gate, key_gate=key_gate, value_input=value_input, out_grad=out_grad, filter_param=filter_param)


def reference(query_gate, key_gate, value_input, out_grad, filter_param):
    size = 2 * L
    scale = L ** -0.5
    taps = filter_param.T * scale
    gated = key_gate * value_input
    conv_grad = out_grad * query_gate
    filt_spec = jnp.fft.rfft(taps, n=size, axis=0)[None]
    gated_spec = jnp.fft.rfft(gated, n=size, axis=1)
    cgrad_spec = jnp.fft.rfft(conv_grad, n=size, axis=1)
    conv_out = jnp.fft.irfft(gated_spec * filt_spec, n=size, axis=1)[:, :L]
    gated_grad = jnp.fft.irfft(jnp.conj(filt_spec) * cgrad_spec, n=size, axis=1)[:, :L]
    filter_terms = jnp.fft.irfft(jnp.conj(gated_spec) * cgrad_spec, n=size, axis=1)[:, :L]
    filter_grad = (jnp.sum(filter_terms, axis=0) * scale).T
    query_grad = out_grad * conv_out
    key_grad = gated_grad * value_input
    value_grad = gated_grad * key_gate
    return query_grad, key_grad, value_grad, filter_grad
```

```python
import jax
import jax.numpy as jnp
import numpy as np
from jax import lax
from jax.experimental import pallas as pl
from jax.experimental.pallas import tpu as pltpu
from jax.sharding import PartitionSpec as P

TOK = 64
SEQ = 4
ROWS = 512
WIDTH = 128
LENGTH = TOK * ROWS
OUTER = 128
INNER = 256
SCALE = LENGTH**-0.5 / LENGTH

f32 = jnp.float32
bf16 = jnp.bfloat16
VMEM = pl.BlockSpec(memory_space=pltpu.VMEM)
SMEM = pl.BlockSpec(memory_space=pltpu.SMEM)


def split_np(table):
    table = table.astype(np.float32)
    high = table.astype(jnp.bfloat16)
    low = (table - high.astype(np.float32)).astype(jnp.bfloat16)
    return high, low


def tables():
    k1 = np.arange(OUTER, dtype=np.float64)[:, None] + 0.25
    j = np.concatenate([np.arange(0, OUTER, 2), np.arange(1, OUTER, 2)]).astype(np.float64)[None, :]
    outer = 2.0 * np.pi * np.mod(k1 * j, OUTER) / OUTER
    w = np.concatenate([np.cos(outer), -np.sin(outer)], axis=0)
    wh, wl = split_np(w)
    w_fwd = np.concatenate([wh, wh, wl], axis=1)
    vh, vl = split_np(w.T)
    w_inv = np.concatenate([vh, vh, vl], axis=1)
    r = np.arange(INNER, dtype=np.float64)[None, :]
    twist = 2.0 * np.pi * k1 * r / LENGTH
    tw = np.stack([np.cos(twist), -np.sin(twist)]).astype(np.float32)
    inner = 2.0 * np.pi * np.mod(r.T * r, INNER) / INNER
    c, s = np.cos(inner), np.sin(inner)
    t = np.block([[c, -s], [s, c]])
    th, tl = split_np(t)
    t_cat = np.concatenate([th, th, tl], axis=0)
    return w_fwd, w_inv, tw, t_cat


def split(value):
    high = value.astype(bf16)
    low = (value - high.astype(f32)).astype(bf16)
    return high, low


def send_kernel(query_ref, key_ref, value_ref, grad_ref, out_ref):
    for q in range(4):
        rows = pl.ds(q * 128, 128)
        gated = key_ref[rows, :] * value_ref[rows, :]
        cgrad = grad_ref[rows, :] * query_ref[rows, :]
        out_ref[pl.ds(q, 128, stride=8), :] = gated.T
        out_ref[pl.ds(4 + q, 128, stride=8), :] = cgrad.T


def spectral_kernel(
    part_ref, recv_ref, f0_ref, f1_ref, f2_ref, f3_ref, wf_ref, wi_ref, tw_ref, t_ref,
    out_ref, g0_ref, g1_ref, g2_ref, g3_ref,
    taps, cat, spec, terms,
):
    for k, f_ref in enumerate((f0_ref, f1_ref, f2_ref, f3_ref)):
        base = part_ref[k] * 16
        for c in range(2):
            for q2 in range(2):
                for h in range(2):
                    taps[c, pl.ds(pl.multiple_of(q2 * 64 + base, 16), 16), pl.ds(h * 128, 128)] = f_ref[
                        pl.ds(4 * q2 + 2 * h + c, 16, stride=8), :
                    ]

    def store_cat(row, left, right):
        lh, ll = split(left)
        rh, rl = split(right)
        rows = pl.ds(row * OUTER, OUTER)
        cat[rows, 0:256] = lh
        cat[rows, 256:512] = rh
        cat[rows, 512:768] = ll
        cat[rows, 768:1024] = rl
        cat[rows, 1024:1280] = lh
        cat[rows, 1280:1536] = rh

    for sig in range(3):
        for c in range(2):
            if sig < 2:
                x = jnp.concatenate(
                    [
                        jnp.concatenate(
                            [recv_ref[pl.ds(c * 8 + sig * 4 + 2 * q2 + h, 64, stride=16), :] for h in range(2)],
                            axis=1,
                        )
                        for q2 in range(2)
                    ],
                    axis=0,
                )
            else:
                x = taps[c]
            xh, xl = split(x)
            a = jnp.dot(wf_ref[...], jnp.concatenate([xh, xl, xh], axis=0), preferred_element_type=f32)
            ar, ai = a[:OUTER], a[OUTER:]
            tr, ti = tw_ref[0], tw_ref[1]
            store_cat(2 * sig + c, ar * tr - ai * ti, ar * ti + ai * tr)

    spec[...] = jnp.dot(cat[...], t_ref[...], preferred_element_type=f32)

    for c in range(2):
        def part(sig, im):
            return spec[pl.ds((2 * sig + c) * OUTER, OUTER), pl.ds(im * INNER, INNER)]

        gr, gi = part(0, 0), part(0, 1)
        cr, ci = part(1, 0), part(1, 1)
        hr, hi = part(2, 0), part(2, 1)
        store_cat(c, gr * hi + gi * hr, gr * hr - gi * hi)
        store_cat(2 + c, hr * ci - hi * cr, hr * cr + hi * ci)
        store_cat(4 + c, gr * ci - gi * cr, gr * cr + gi * ci)

    spec[...] = jnp.dot(cat[...], t_ref[...], preferred_element_type=f32)

    for sig in range(3):
        for c in range(2):
            rows = pl.ds((2 * sig + c) * OUTER, OUTER)
            di, dr = spec[rows, 0:INNER], spec[rows, INNER : 2 * INNER]
            tr, ti = tw_ref[0], tw_ref[1]
            e = jnp.concatenate([dr * tr + di * ti, di * tr - dr * ti], axis=0)
            eh, el = split(e)
            y = jnp.dot(wi_ref[...], jnp.concatenate([eh, el, eh], axis=0), preferred_element_type=f32)
            y = y * SCALE
            for q2 in range(2):
                for h in range(2):
                    block = y[q2 * 64 : q2 * 64 + 64, h * 128 : h * 128 + 128]
                    if sig < 2:
                        out_ref[pl.ds(c * 8 + sig * 4 + 2 * q2 + h, 64, stride=16), :] = block
                    else:
                        terms[pl.ds(4 * q2 + 2 * h + c, 64, stride=8), :] = block
    for k, g_ref in enumerate((g0_ref, g1_ref, g2_ref, g3_ref)):
        g_ref[...] = terms[pl.ds(pl.multiple_of(part_ref[k] * 128, 128), 128), :]


def finish_kernel(
    recv_ref, query_ref, key_ref, value_ref, grad_ref, g0_ref, g1_ref, g2_ref, g3_ref,
    qg_ref, kg_ref, vg_ref, fg_ref,
):
    for q in range(4):
        rows = pl.ds(q * 128, 128)
        conv = recv_ref[pl.ds(q, 128, stride=8), :].T
        ggrad = recv_ref[pl.ds(4 + q, 128, stride=8), :].T
        qg_ref[rows, :] = grad_ref[rows, :] * conv
        kg_ref[rows, :] = ggrad * value_ref[rows, :]
        vg_ref[rows, :] = ggrad * key_ref[rows, :]
    fg_ref[...] = (g0_ref[...] + g1_ref[...]) + (g2_ref[...] + g3_ref[...])


def shape(*dims, kind=f32):
    return jax.ShapeDtypeStruct(dims, kind)


def body(query_gate, key_gate, value_input, out_grad, filter_param):
    query, key, value, grad = (a.reshape(ROWS, WIDTH) for a in (query_gate, key_gate, value_input, out_grad))
    me = lax.axis_index("seq")
    parts = jnp.bitwise_xor(me, jnp.arange(SEQ, dtype=jnp.int32)).astype(jnp.int32)

    def swap(block, k):
        return lax.ppermute(block, "seq", [(s, s ^ k) for s in range(SEQ)])

    own = filter_param.reshape(2, 64, 128).transpose(1, 0, 2).reshape(128, 128)
    pieces = [own] + [swap(own, k) for k in (1, 2, 3)]
    sent = pl.pallas_call(
        send_kernel,
        out_shape=shape(TOK * 16, 128),
        in_specs=[VMEM] * 4,
        out_specs=VMEM,
        name="send",
    )(query, key, value, grad)
    recv = lax.all_to_all(sent.reshape(TOK, 16, 128), "tok", split_axis=0, concat_axis=0, tiled=True)
    w_fwd, w_inv, tw, t_cat = tables()
    back, *grads = pl.pallas_call(
        spectral_kernel,
        out_shape=(shape(TOK * 16, 128), *[shape(128, 128)] * 4),
        in_specs=[SMEM] + [VMEM] * 9,
        out_specs=(VMEM,) * 5,
        scratch_shapes=[
            pltpu.VMEM((2, OUTER, INNER), f32),
            pltpu.VMEM((6 * OUTER, 6 * INNER), bf16),
            pltpu.VMEM((6 * OUTER, 2 * INNER), f32),
            pltpu.VMEM((SEQ * 128, 128), f32),
        ],
        name="spectral",
    )(parts, recv.reshape(TOK * 16, 128), *pieces, w_fwd, w_inv, tw, t_cat)
    terms = [grads[0]] + [swap(grads[k], k) for k in (1, 2, 3)]
    home = lax.all_to_all(back.reshape(TOK, 16, 128), "tok", split_axis=0, concat_axis=0, tiled=True)
    qg, kg, vg, fg = pl.pallas_call(
        finish_kernel,
        out_shape=(*[shape(ROWS, WIDTH)] * 3, shape(128, 128)),
        in_specs=[VMEM] * 9,
        out_specs=(VMEM,) * 4,
        name="finish",
    )(home.reshape(TOK * 16, 128), query, key, value, grad, *terms)
    filter_grad = fg.reshape(64, 2, 128).transpose(1, 0, 2).reshape(2, 8192)
    return (qg[None], kg[None], vg[None], filter_grad)


def solution(mesh):
    tokens = P("seq", "tok", None)
    taps = P("tok", "seq")
    return jax.shard_map(
        body,
        mesh=mesh,
        in_specs=(tokens, tokens, tokens, tokens, taps),
        out_specs=(tokens, tokens, tokens, taps),
        check_vma=False,
    )
```

```python
import jax
import jax.numpy as jnp
import numpy as np
from jax import lax
from jax.experimental import pallas as pl
from jax.experimental.pallas import tpu as pltpu
from jax.sharding import PartitionSpec as P

TOK = 64
SEQ = 4
ROWS = 512
WIDTH = 128
LENGTH = TOK * ROWS
OUTER = 128
INNER = 256
HALF = INNER // 2
SCALE = LENGTH**-0.5 / LENGTH

PIECE = (0, 2, 1, 3)

f32 = jnp.float32
bf16 = jnp.bfloat16
VMEM = pl.BlockSpec(memory_space=pltpu.VMEM)
HBM = pl.BlockSpec(memory_space=pltpu.HBM)
SMEM = pl.BlockSpec(memory_space=pltpu.SMEM)


def split_np(table):
    table = table.astype(np.float32)
    high = table.astype(jnp.bfloat16)
    low = (table - high.astype(np.float32)).astype(jnp.bfloat16)
    return high, low


def stack_np(real, imag, left):
    high, low = split_np(np.block([[real, imag], [-imag, real]]))
    return np.concatenate([high, high, low], axis=1 if left else 0)


def tables():
    k1 = np.arange(OUTER, dtype=np.float64)[:, None] + 0.25
    j = np.concatenate([np.arange(0, OUTER, 2), np.arange(1, OUTER, 2)]).astype(np.float64)[None, :]
    outer = 2.0 * np.pi * np.mod(k1 * j, OUTER) / OUTER
    w = np.concatenate([np.cos(outer), -np.sin(outer)], axis=0)
    wh, wl = split_np(w)
    w_fwd = np.concatenate([wh, wh, wl], axis=1)
    vh, vl = split_np(w.T)
    w_inv = np.concatenate([vh, vh, vl], axis=1)
    r = np.arange(INNER, dtype=np.float64)[None, :]
    twist = 2.0 * np.pi * k1 * r / LENGTH
    tw = np.stack([np.cos(twist), -np.sin(twist)]).astype(np.float32)
    l = np.arange(HALF, dtype=np.float64)[:, None]
    m = np.arange(HALF, dtype=np.float64)[None, :]
    even = 2.0 * np.pi * np.mod(l * 2 * m, INNER) / INNER
    odd = 2.0 * np.pi * np.mod(l * (2 * m + 1), INNER) / INNER
    t_even = stack_np(np.cos(even), -np.sin(even), False)
    t_odd = stack_np(np.cos(odd), -np.sin(odd), False)
    t_back = stack_np(np.cos(odd.T), -np.sin(odd.T), False)
    return w_fwd, w_inv, tw, t_even, t_odd, t_back


def split(value):
    high = value.astype(bf16)
    low = (value - high.astype(f32)).astype(bf16)
    return high, low


def send_kernel(query_hbm, key_hbm, value_hbm, grad_hbm, out_hbm, query, key, value, grad, tiles, sem, out_sem):
    pairs = ((query_hbm, query), (key_hbm, key), (value_hbm, value), (grad_hbm, grad))
    copies, sends = [], []
    for q in range(4):
        rows = pl.ds(q * 128, 128)
        copies.append([pltpu.make_async_copy(a.at[rows], b.at[rows], sem.at[q, i]) for i, (a, b) in enumerate(pairs)])
        for copy in copies[q]:
            copy.start()
    for q in range(4):
        rows = pl.ds(q * 128, 128)
        for copy in copies[q]:
            copy.wait()
        tiles[q] = (key[rows, :] * value[rows, :]).T
        tiles[4 + q] = (grad[rows, :] * query[rows, :]).T
        for i in (q, 4 + q):
            sends.append(pltpu.make_async_copy(tiles.at[i], out_hbm.at[:, i, :], out_sem.at[i]))
            sends[-1].start()
    for send in sends:
        send.wait()


def store_cat(cat, row, left, right):
    lh, ll = split(left)
    rh, rl = split(right)
    rows = pl.ds(row * OUTER, OUTER)
    cat[rows, 0:128] = lh
    cat[rows, 128:256] = rh
    cat[rows, 256:384] = ll
    cat[rows, 384:512] = rl
    cat[rows, 512:640] = lh
    cat[rows, 640:768] = rh


def forward_outer(x, row, wf_ref, tw_ref, cat_e, cat_o):
    xh, xl = split(x)
    a = jnp.dot(wf_ref[...], jnp.concatenate([xh, xl, xh], axis=0), preferred_element_type=f32)
    ar, ai = a[:OUTER], a[OUTER:]
    tr, ti = tw_ref[0], tw_ref[1]
    br, bi = ar * tr - ai * ti, ar * ti + ai * tr
    store_cat(cat_e, row, br[:, :HALF] + br[:, HALF:], bi[:, :HALF] + bi[:, HALF:])
    store_cat(cat_o, row, br[:, :HALF] - br[:, HALF:], bi[:, :HALF] - bi[:, HALF:])


def inverse_outer(spec_e, spec_o, row, wi_ref, tw_ref):
    rows = pl.ds(row * OUTER, OUTER)
    ei, er = spec_e[rows, 0:HALF], spec_e[rows, HALF : 2 * HALF]
    oi, orr = spec_o[rows, 0:HALF], spec_o[rows, HALF : 2 * HALF]
    dr = jnp.concatenate([er + orr, er - orr], axis=1)
    di = jnp.concatenate([ei + oi, ei - oi], axis=1)
    tr, ti = tw_ref[0], tw_ref[1]
    e = jnp.concatenate([dr * tr + di * ti, di * tr - dr * ti], axis=0)
    eh, el = split(e)
    y = jnp.dot(wi_ref[...], jnp.concatenate([eh, el, eh], axis=0), preferred_element_type=f32)
    return y * SCALE


def matmul(cat, table):
    return jnp.dot(cat[...], table[...], preferred_element_type=f32)


def taps_kernel(
    part_ref, near_ref, far_ref, wf_ref, tw_ref, te_ref, to_ref, out_hbm, taps, cat_e, cat_o, spec, sem
):
    for k in range(SEQ):
        f_ref, first = (near_ref if k < 2 else far_ref), (k % 2) * 128
        base = part_ref[PIECE[k]] * 16
        for c in range(2):
            for q2 in range(2):
                for h in range(2):
                    taps[c, pl.ds(pl.multiple_of(q2 * 64 + base, 16), 16), pl.ds(h * 128, 128)] = f_ref[
                        pl.ds(first + 4 * q2 + 2 * h + c, 16, stride=8), :
                    ]
    for c in range(2):
        forward_outer(taps[c], c, wf_ref, tw_ref, cat_e, cat_o)
    copies = []
    for p, (cat, t_ref) in enumerate(((cat_e, te_ref), (cat_o, to_ref))):
        spec[p] = matmul(cat, t_ref)
        copies.append(pltpu.make_async_copy(spec.at[p], out_hbm.at[p], sem.at[p]))
        copies[p].start()
    for copy in copies:
        copy.wait()


def spectral_kernel(
    recv_ref, taps_ref, wf_ref, wi_ref, tw_ref, te_ref, to_ref, tb_ref,
    out_hbm, cross_hbm,
    cat_e, cat_o, spec_e, spec_o, cross, tiles, sem, out_sem,
):
    for sig in range(2):
        for c in range(2):
            x = jnp.concatenate(
                [
                    jnp.concatenate(
                        [recv_ref[pl.ds(c * 8 + sig * 4 + 2 * q2 + h, 64, stride=16), :] for h in range(2)],
                        axis=1,
                    )
                    for q2 in range(2)
                ],
                axis=0,
            )
            forward_outer(x, 2 * sig + c, wf_ref, tw_ref, cat_e, cat_o)

    spec_e[...] = matmul(cat_e, te_ref)
    spec_o[...] = matmul(cat_o, to_ref)

    for p, (cat, spec) in enumerate(((cat_e, spec_e), (cat_o, spec_o))):
        for c in range(2):
            def part(ref, row, im):
                return ref[pl.ds(row * OUTER, OUTER), pl.ds(im * HALF, HALF)]

            gr, gi = part(spec, c, 0), part(spec, c, 1)
            cr, ci = part(spec, 2 + c, 0), part(spec, 2 + c, 1)
            hr, hi = part(taps_ref.at[p], c, 0), part(taps_ref.at[p], c, 1)
            store_cat(cat, c, gr * hi + gi * hr, gr * hr - gi * hi)
            store_cat(cat, 2 + c, hr * ci - hi * cr, hr * cr + hi * ci)
            cross[p, pl.ds(c * OUTER, OUTER), 0:HALF] = gr * ci - gi * cr
            cross[p, pl.ds(c * OUTER, OUTER), HALF : 2 * HALF] = gr * cr + gi * ci

    sends = [pltpu.make_async_copy(cross, cross_hbm, sem)]
    sends[0].start()
    spec_e[...] = matmul(cat_e, te_ref)
    spec_o[...] = matmul(cat_o, tb_ref)

    for sig in range(2):
        for c in range(2):
            y = inverse_outer(spec_e, spec_o, 2 * sig + c, wi_ref, tw_ref)
            for q2 in range(2):
                for h in range(2):
                    i = c * 8 + sig * 4 + 2 * q2 + h
                    tiles[i] = y[q2 * 64 : q2 * 64 + 64, h * 128 : h * 128 + 128]
                    sends.append(pltpu.make_async_copy(tiles.at[i], out_hbm.at[:, i, :], out_sem.at[i]))
                    sends[-1].start()
    for send in sends:
        send.wait()


def terms_kernel(
    part_ref, cross_ref, wi_ref, tw_ref, te_ref, tb_ref, own_ref, give_ref, cat_e, cat_o, spec_e, spec_o, terms
):
    for p, cat in enumerate((cat_e, cat_o)):
        for c in range(2):
            rows = pl.ds(c * OUTER, OUTER)
            store_cat(cat, c, cross_ref[p, rows, 0:HALF], cross_ref[p, rows, HALF : 2 * HALF])
    spec_e[...] = matmul(cat_e, te_ref)
    spec_o[...] = matmul(cat_o, tb_ref)
    for c in range(2):
        y = inverse_outer(spec_e, spec_o, c, wi_ref, tw_ref)
        for q2 in range(2):
            for h in range(2):
                terms[pl.ds(4 * q2 + 2 * h + c, 64, stride=8), :] = y[
                    q2 * 64 : q2 * 64 + 64, h * 128 : h * 128 + 128
                ]
    for k in range(SEQ):
        ref, first = (own_ref if k < 2 else give_ref), (k % 2) * 128
        ref[first : first + 128, :] = terms[
            pl.ds(pl.multiple_of(part_ref[PIECE[k]] * 128, 128), 128), :
        ]


def finish_kernel(
    recv_ref, query_ref, key_ref, value_ref, grad_ref, own_ref, far_ref,
    qg_hbm, kg_hbm, vg_hbm, fg_hbm,
    qg, kg, vg, fg, sem,
):
    fg[...] = own_ref[...] + far_ref[...]
    copies = [pltpu.make_async_copy(fg, fg_hbm, sem.at[12])]
    copies[0].start()
    for q in range(4):
        rows = pl.ds(q * 128, 128)
        conv = recv_ref[pl.ds(q, 128, stride=8), :].T
        ggrad = recv_ref[pl.ds(4 + q, 128, stride=8), :].T
        qg[rows, :] = grad_ref[rows, :] * conv
        kg[rows, :] = ggrad * value_ref[rows, :]
        vg[rows, :] = ggrad * key_ref[rows, :]
        for i, (a, b) in enumerate(((qg, qg_hbm), (kg, kg_hbm), (vg, vg_hbm))):
            copy = pltpu.make_async_copy(a.at[rows], b.at[rows], sem.at[3 * q + i])
            copy.start()
            copies.append(copy)
    for copy in copies:
        copy.wait()


def shape(*dims, kind=f32):
    return jax.ShapeDtypeStruct(dims, kind)


def room(mib):
    return pltpu.CompilerParams(vmem_limit_bytes=mib * 2**20)


def cost(units):
    return pl.CostEstimate(flops=units * 800_000_000, bytes_accessed=units * 1_000_000, transcendentals=0)


def body(query_gate, key_gate, value_input, out_grad, filter_param):
    query, key, value, grad = (a.reshape(ROWS, WIDTH) for a in (query_gate, key_gate, value_input, out_grad))
    me = lax.axis_index("seq")
    parts = jnp.bitwise_xor(me, jnp.arange(SEQ, dtype=jnp.int32)).astype(jnp.int32)

    def swap(block, k):
        return lax.ppermute(block, "seq", [(s, s ^ k) for s in range(SEQ)])

    own = filter_param.reshape(2, 64, 128).transpose(1, 0, 2).reshape(128, 128)
    near = jnp.concatenate([own, swap(own, 2)], axis=0)
    far = swap(near, 1)
    w_fwd, w_inv, tw, t_even, t_odd, t_back = tables()
    sent = pl.pallas_call(
        send_kernel,
        out_shape=shape(TOK * 2, 8, 128),
        in_specs=[HBM] * 4,
        out_specs=HBM,
        scratch_shapes=[pltpu.VMEM((ROWS, WIDTH), f32)] * 4
        + [pltpu.VMEM((8, 128, 128), f32), pltpu.SemaphoreType.DMA((4, 4)), pltpu.SemaphoreType.DMA((8,))],
        compiler_params=room(60),
        name="send",
    )(query, key, value, grad)
    recv = lax.all_to_all(sent.reshape(TOK, 16, 128), "tok", split_axis=0, concat_axis=0, tiled=True)
    taps = pl.pallas_call(
        taps_kernel,
        out_shape=shape(2, 2 * OUTER, INNER),
        in_specs=[SMEM] + [VMEM] * 6,
        out_specs=HBM,
        scratch_shapes=[pltpu.VMEM((2, OUTER, INNER), f32)]
        + [pltpu.VMEM((2 * OUTER, 3 * INNER), bf16)] * 2
        + [pltpu.VMEM((2, 2 * OUTER, INNER), f32), pltpu.SemaphoreType.DMA((2,))],
        compiler_params=room(8),
        cost_estimate=cost(1),
        name="taps",
    )(parts, near, far, w_fwd, tw, t_even, t_odd)
    back, cross = pl.pallas_call(
        spectral_kernel,
        out_shape=(shape(TOK, 16, 128), pltpu.HBM((2, 2 * OUTER, INNER), f32)),
        in_specs=[VMEM] * 8,
        out_specs=(HBM, HBM),
        scratch_shapes=[pltpu.VMEM((4 * OUTER, 3 * INNER), bf16)] * 2
        + [pltpu.VMEM((4 * OUTER, INNER), f32)] * 2
        + [pltpu.VMEM((2, 2 * OUTER, INNER), f32)]
        + [pltpu.VMEM((16, TOK, 128), f32), pltpu.SemaphoreType.DMA, pltpu.SemaphoreType.DMA((16,))],
        compiler_params=room(8),
        cost_estimate=cost(4),
        name="spectral",
    )(recv.reshape(TOK * 16, 128), taps, w_fwd, w_inv, tw, t_even, t_odd, t_back)
    home = lax.all_to_all(back.reshape(TOK, 16, 128), "tok", split_axis=0, concat_axis=0, tiled=True)
    kept, given = pl.pallas_call(
        terms_kernel,
        out_shape=(shape(256, 128),) * 2,
        in_specs=[SMEM] + [VMEM] * 5,
        out_specs=(VMEM,) * 2,
        scratch_shapes=[pltpu.VMEM((2 * OUTER, 3 * INNER), bf16)] * 2
        + [pltpu.VMEM((2 * OUTER, INNER), f32)] * 2
        + [pltpu.VMEM((SEQ * 128, 128), f32)],
        compiler_params=room(8),
        cost_estimate=cost(1),
        name="terms",
    )(parts, cross, w_inv, tw, t_even, t_back)
    paired = kept + swap(given, 1)
    terms = (paired[:128], swap(paired[128:], 2))
    qg, kg, vg, fg = pl.pallas_call(
        finish_kernel,
        out_shape=(*[shape(ROWS, WIDTH)] * 3, shape(128, 128)),
        in_specs=[VMEM] * 7,
        out_specs=(HBM,) * 4,
        scratch_shapes=[pltpu.VMEM((ROWS, WIDTH), f32)] * 3
        + [pltpu.VMEM((128, 128), f32), pltpu.SemaphoreType.DMA((13,))],
        compiler_params=room(8),
        name="finish",
    )(home.reshape(TOK * 16, 128), query, key, value, grad, *terms)
    filter_grad = fg.reshape(64, 2, 128).transpose(1, 0, 2).reshape(2, 8192)
    return (qg[None], kg[None], vg[None], filter_grad)


def solution(mesh):
    tokens = P("seq", "tok", None)
    taps = P("tok", "seq")
    return jax.shard_map(
        body,
        mesh=mesh,
        in_specs=(tokens, tokens, tokens, tokens, taps),
        out_specs=(tokens, tokens, tokens, taps),
        check_vma=False,
    )
```

```python
import jax
import jax.numpy as jnp
import numpy as np
from jax import lax
from jax.experimental import pallas as pl
from jax.experimental.pallas import tpu as pltpu
from jax.sharding import PartitionSpec as P

TOK = 64
SEQ = 4
ROWS = 512
WIDTH = 128
LENGTH = TOK * ROWS
OUTER = 128
INNER = 256
HALF = INNER // 2
CHUNK = 16
SCALE = LENGTH**-0.5 / LENGTH

PIECE = (0, 2, 1, 3)

f32 = jnp.float32
bf16 = jnp.bfloat16
VMEM = pl.BlockSpec(memory_space=pltpu.VMEM)
HBM = pl.BlockSpec(memory_space=pltpu.HBM)
SMEM = pl.BlockSpec(memory_space=pltpu.SMEM)


def split_np(table):
    table = table.astype(np.float32)
    high = table.astype(jnp.bfloat16)
    low = (table - high.astype(np.float32)).astype(jnp.bfloat16)
    return high, low


def stack_np(real, imag, left):
    high, low = split_np(np.block([[real, imag], [-imag, real]]))
    return np.concatenate([high, high, low], axis=1 if left else 0)


def tables():
    k1 = np.arange(OUTER, dtype=np.float64)[:, None] + 0.25
    j = np.concatenate([np.arange(0, OUTER, 2), np.arange(1, OUTER, 2)]).astype(np.float64)[None, :]
    outer = 2.0 * np.pi * np.mod(k1 * j, OUTER) / OUTER
    w = np.stack([np.cos(outer), -np.sin(outer)]).reshape(2, OUTER // CHUNK, CHUNK, OUTER)
    w = w.transpose(1, 0, 2, 3).reshape(2 * OUTER, OUTER)
    wh, wl = split_np(w)
    w_fwd = np.concatenate([wh, wh, wl], axis=1)
    vh, vl = split_np(w.T * SCALE)
    w_inv = np.concatenate([vh, vh, vl], axis=1)
    r = np.arange(INNER, dtype=np.float64)[None, :]
    twist = 2.0 * np.pi * k1 * r / LENGTH
    tw = np.stack([np.cos(twist), -np.sin(twist)]).astype(np.float32)
    l = np.arange(HALF, dtype=np.float64)[:, None]
    m = np.arange(HALF, dtype=np.float64)[None, :]
    even = 2.0 * np.pi * np.mod(l * 2 * m, INNER) / INNER
    odd = 2.0 * np.pi * np.mod(l * (2 * m + 1), INNER) / INNER
    t_even = stack_np(np.cos(even), -np.sin(even), False)
    t_odd = stack_np(np.cos(odd), -np.sin(odd), False)
    t_back = stack_np(np.cos(odd.T), -np.sin(odd.T), False)
    return w_fwd, w_inv, tw, t_even, t_odd, t_back


def split(value):
    high = value.astype(bf16)
    low = (value - high.astype(f32)).astype(bf16)
    return high, low


def send_kernel(query_hbm, key_hbm, value_hbm, grad_hbm, out_hbm, query, key, value, grad, tiles, sem, out_sem):
    pairs = ((query_hbm, query), (key_hbm, key), (value_hbm, value), (grad_hbm, grad))
    copies, sends = [], []
    for q in range(4):
        rows = pl.ds(q * 128, 128)
        copies.append([pltpu.make_async_copy(a.at[rows], b.at[rows], sem.at[q, i]) for i, (a, b) in enumerate(pairs)])
        for copy in copies[q]:
            copy.start()
    for q in range(4):
        rows = pl.ds(q * 128, 128)
        for copy in copies[q]:
            copy.wait()
        tiles[q] = (key[rows, :] * value[rows, :]).T
        tiles[4 + q] = (grad[rows, :] * query[rows, :]).T
        for i in (q, 4 + q):
            sends.append(pltpu.make_async_copy(tiles.at[i], out_hbm.at[:, i, :], out_sem.at[i]))
            sends[-1].start()
    for send in sends:
        send.wait()


def store_cat(cat, first, left, right):
    lh, ll = split(left)
    rh, rl = split(right)
    rows = pl.ds(first, left.shape[0])
    cat[rows, 0:128] = lh
    cat[rows, 128:256] = rh
    cat[rows, 256:384] = ll
    cat[rows, 384:512] = rl
    cat[rows, 512:640] = lh
    cat[rows, 640:768] = rh


def forward_outer(x, row, wf_ref, tw_ref, cat_e, cat_o):
    xh, xl = split(x)
    a = jnp.dot(wf_ref[...], jnp.concatenate([xh, xl, xh], axis=0), preferred_element_type=f32)
    for i in range(0, OUTER, CHUNK):
        ar, ai = a[2 * i : 2 * i + CHUNK], a[2 * i + CHUNK : 2 * i + 2 * CHUNK]
        tr, ti = tw_ref[0, i : i + CHUNK, :], tw_ref[1, i : i + CHUNK, :]
        br, bi = ar * tr - ai * ti, ar * ti + ai * tr
        first = row * OUTER + i
        store_cat(cat_e, first, br[:, :HALF] + br[:, HALF:], bi[:, :HALF] + bi[:, HALF:])
        store_cat(cat_o, first, br[:, :HALF] - br[:, HALF:], bi[:, :HALF] - bi[:, HALF:])


def inverse_outer(spec_e, spec_o, row, wi_ref, tw_ref, cat):
    for i in range(0, OUTER, CHUNK):
        rows = pl.ds(row * OUTER + i, CHUNK)
        ei, er = spec_e[rows, 0:HALF], spec_e[rows, HALF : 2 * HALF]
        oi, orr = spec_o[rows, 0:HALF], spec_o[rows, HALF : 2 * HALF]
        dr = jnp.concatenate([er + orr, er - orr], axis=1)
        di = jnp.concatenate([ei + oi, ei - oi], axis=1)
        tr, ti = tw_ref[0, i : i + CHUNK, :], tw_ref[1, i : i + CHUNK, :]
        for first, e in ((2 * i, dr * tr + di * ti), (2 * i + CHUNK, di * tr - dr * ti)):
            eh, el = split(e)
            cat[pl.ds(first, CHUNK), :] = eh
            cat[pl.ds(256 + first, CHUNK), :] = el
            cat[pl.ds(512 + first, CHUNK), :] = eh
    return matmul(wi_ref, cat)


def matmul(cat, table):
    return jnp.dot(cat[...], table[...], preferred_element_type=f32)


def taps_kernel(
    part_ref, near_ref, far_ref, wf_ref, tw_ref, te_ref, to_ref, out_hbm, taps, cat_e, cat_o, spec, sem
):
    for k in range(SEQ):
        f_ref, first = (near_ref if k < 2 else far_ref), (k % 2) * 128
        base = part_ref[PIECE[k]] * 16
        for c in range(2):
            for q2 in range(2):
                for h in range(2):
                    taps[c, pl.ds(pl.multiple_of(q2 * 64 + base, 16), 16), pl.ds(h * 128, 128)] = f_ref[
                        pl.ds(first + 4 * q2 + 2 * h + c, 16, stride=8), :
                    ]
    for c in range(2):
        forward_outer(taps[c], c, wf_ref, tw_ref, cat_e, cat_o)
    copies = []
    for p, (cat, t_ref) in enumerate(((cat_e, te_ref), (cat_o, to_ref))):
        spec[p] = matmul(cat, t_ref)
        copies.append(pltpu.make_async_copy(spec.at[p], out_hbm.at[p], sem.at[p]))
        copies[p].start()
    for copy in copies:
        copy.wait()


def spectral_kernel(
    recv_ref, taps_ref, wf_ref, wi_ref, tw_ref, te_ref, to_ref, tb_ref,
    out_hbm, cross_hbm,
    cat_e, cat_o, spec_e, spec_o, back, cross, tiles, sem, out_sem,
):
    sends = []
    for c in range(2):
        for sig in range(2):
            x = jnp.concatenate(
                [
                    jnp.concatenate(
                        [recv_ref[pl.ds(c * 8 + sig * 4 + 2 * q2 + h, 64, stride=16), :] for h in range(2)],
                        axis=1,
                    )
                    for q2 in range(2)
                ],
                axis=0,
            )
            forward_outer(x, 2 * c + sig, wf_ref, tw_ref, cat_e, cat_o)

    def product(p, cat, spec):
        for c in range(2):
            for i in range(0, OUTER, CHUNK):
                g, k = pl.ds(2 * c * OUTER + i, CHUNK), pl.ds((2 * c + 1) * OUTER + i, CHUNK)
                h = pl.ds(c * OUTER + i, CHUNK)
                gr, gi = spec[g, 0:HALF], spec[g, HALF : 2 * HALF]
                cr, ci = spec[k, 0:HALF], spec[k, HALF : 2 * HALF]
                hr, hi = taps_ref[p, h, 0:HALF], taps_ref[p, h, HALF : 2 * HALF]
                store_cat(cat, 2 * c * OUTER + i, gr * hi + gi * hr, gr * hr - gi * hi)
                store_cat(cat, (2 * c + 1) * OUTER + i, hr * ci - hi * cr, hr * cr + hi * ci)
                cross[p, h, 0:HALF] = gr * ci - gi * cr
                cross[p, h, HALF : 2 * HALF] = gr * cr + gi * ci

    spec_e[...] = matmul(cat_e, te_ref)
    spec_o[...] = matmul(cat_o, to_ref)
    product(0, cat_e, spec_e)
    spec_e[...] = matmul(cat_e, te_ref)
    product(1, cat_o, spec_o)
    sends.append(pltpu.make_async_copy(cross, cross_hbm, sem))
    sends[0].start()
    spec_o[...] = matmul(cat_o, tb_ref)

    for c in range(2):
        for sig in range(2):
            y = inverse_outer(spec_e, spec_o, 2 * c + sig, wi_ref, tw_ref, back.at[2 * c + sig])
            for q2 in range(2):
                for h in range(2):
                    i = c * 8 + sig * 4 + 2 * q2 + h
                    tiles[i] = y[q2 * 64 : q2 * 64 + 64, h * 128 : h * 128 + 128]
                    sends.append(pltpu.make_async_copy(tiles.at[i], out_hbm.at[:, i, :], out_sem.at[i]))
                    sends[-1].start()
    for send in sends:
        send.wait()


def terms_kernel(
    part_ref, cross_ref, wi_ref, tw_ref, te_ref, tb_ref, own_ref, give_ref, cat_e, cat_o, spec_e, spec_o, back, terms
):
    for p, cat in enumerate((cat_e, cat_o)):
        for c in range(2):
            rows = pl.ds(c * OUTER, OUTER)
            store_cat(cat, c * OUTER, cross_ref[p, rows, 0:HALF], cross_ref[p, rows, HALF : 2 * HALF])
    spec_e[...] = matmul(cat_e, te_ref)
    spec_o[...] = matmul(cat_o, tb_ref)
    for c in range(2):
        y = inverse_outer(spec_e, spec_o, c, wi_ref, tw_ref, back.at[c])
        for q2 in range(2):
            for h in range(2):
                terms[pl.ds(4 * q2 + 2 * h + c, 64, stride=8), :] = y[
                    q2 * 64 : q2 * 64 + 64, h * 128 : h * 128 + 128
                ]
    for k in range(SEQ):
        ref, first = (own_ref if k < 2 else give_ref), (k % 2) * 128
        ref[first : first + 128, :] = terms[
            pl.ds(pl.multiple_of(part_ref[PIECE[k]] * 128, 128), 128), :
        ]


def finish_kernel(
    recv_ref, query_ref, key_ref, value_ref, grad_ref, own_ref, far_ref,
    qg_hbm, kg_hbm, vg_hbm, fg_hbm,
    qg, kg, vg, fg, sem,
):
    fg[...] = own_ref[...] + far_ref[...]
    copies = [pltpu.make_async_copy(fg, fg_hbm, sem.at[12])]
    copies[0].start()
    for q in range(4):
        rows = pl.ds(q * 128, 128)
        conv = recv_ref[pl.ds(q, 128, stride=8), :].T
        ggrad = recv_ref[pl.ds(4 + q, 128, stride=8), :].T
        qg[rows, :] = grad_ref[rows, :] * conv
        kg[rows, :] = ggrad * value_ref[rows, :]
        vg[rows, :] = ggrad * key_ref[rows, :]
        for i, (a, b) in enumerate(((qg, qg_hbm), (kg, kg_hbm), (vg, vg_hbm))):
            copy = pltpu.make_async_copy(a.at[rows], b.at[rows], sem.at[3 * q + i])
            copy.start()
            copies.append(copy)
    for copy in copies:
        copy.wait()


def shape(*dims, kind=f32):
    return jax.ShapeDtypeStruct(dims, kind)


def room(mib):
    return pltpu.CompilerParams(vmem_limit_bytes=mib * 2**20)


def cost(units):
    return pl.CostEstimate(flops=units * 800_000_000, bytes_accessed=units * 1_000_000, transcendentals=0)


def body(query_gate, key_gate, value_input, out_grad, filter_param):
    query, key, value, grad = (a.reshape(ROWS, WIDTH) for a in (query_gate, key_gate, value_input, out_grad))
    me = lax.axis_index("seq")
    parts = jnp.bitwise_xor(me, jnp.arange(SEQ, dtype=jnp.int32)).astype(jnp.int32)

    def swap(block, k):
        return lax.ppermute(block, "seq", [(s, s ^ k) for s in range(SEQ)])

    own = filter_param.reshape(2, 64, 128).transpose(1, 0, 2).reshape(128, 128)
    near = jnp.concatenate([own, swap(own, 2)], axis=0)
    far = swap(near, 1)
    w_fwd, w_inv, tw, t_even, t_odd, t_back = tables()
    sent = pl.pallas_call(
        send_kernel,
        out_shape=shape(TOK * 2, 8, 128),
        in_specs=[HBM] * 4,
        out_specs=HBM,
        scratch_shapes=[pltpu.VMEM((ROWS, WIDTH), f32)] * 4
        + [pltpu.VMEM((8, 128, 128), f32), pltpu.SemaphoreType.DMA((4, 4)), pltpu.SemaphoreType.DMA((8,))],
        compiler_params=room(60),
        name="send",
    )(query, key, value, grad)
    recv = lax.all_to_all(sent.reshape(TOK, 16, 128), "tok", split_axis=0, concat_axis=0, tiled=True)
    taps = pl.pallas_call(
        taps_kernel,
        out_shape=shape(2, 2 * OUTER, INNER),
        in_specs=[SMEM] + [VMEM] * 6,
        out_specs=HBM,
        scratch_shapes=[pltpu.VMEM((2, OUTER, INNER), f32)]
        + [pltpu.VMEM((2 * OUTER, 3 * INNER), bf16)] * 2
        + [pltpu.VMEM((2, 2 * OUTER, INNER), f32), pltpu.SemaphoreType.DMA((2,))],
        compiler_params=room(8),
        cost_estimate=cost(1),
        name="taps",
    )(parts, near, far, w_fwd, tw, t_even, t_odd)
    back, cross = pl.pallas_call(
        spectral_kernel,
        out_shape=(shape(TOK, 16, 128), pltpu.HBM((2, 2 * OUTER, INNER), f32)),
        in_specs=[VMEM] * 8,
        out_specs=(HBM, HBM),
        scratch_shapes=[pltpu.VMEM((4 * OUTER, 3 * INNER), bf16)] * 2
        + [pltpu.VMEM((4 * OUTER, INNER), f32)] * 2
        + [pltpu.VMEM((4, 6 * OUTER, INNER), bf16), pltpu.VMEM((2, 2 * OUTER, INNER), f32)]
        + [pltpu.VMEM((16, TOK, 128), f32), pltpu.SemaphoreType.DMA, pltpu.SemaphoreType.DMA((16,))],
        compiler_params=room(8),
        cost_estimate=cost(4),
        name="spectral",
    )(recv.reshape(TOK * 16, 128), taps, w_fwd, w_inv, tw, t_even, t_odd, t_back)
    home = lax.all_to_all(back.reshape(TOK, 16, 128), "tok", split_axis=0, concat_axis=0, tiled=True)
    kept, given = pl.pallas_call(
        terms_kernel,
        out_shape=(shape(256, 128),) * 2,
        in_specs=[SMEM] + [VMEM] * 5,
        out_specs=(VMEM,) * 2,
        scratch_shapes=[pltpu.VMEM((2 * OUTER, 3 * INNER), bf16)] * 2
        + [pltpu.VMEM((2 * OUTER, INNER), f32)] * 2
        + [pltpu.VMEM((2, 6 * OUTER, INNER), bf16), pltpu.VMEM((SEQ * 128, 128), f32)],
        compiler_params=room(8),
        cost_estimate=cost(1),
        name="terms",
    )(parts, cross, w_inv, tw, t_even, t_back)
    paired = kept + swap(given, 1)
    terms = (paired[:128], swap(paired[128:], 2))
    qg, kg, vg, fg = pl.pallas_call(
        finish_kernel,
        out_shape=(*[shape(ROWS, WIDTH)] * 3, shape(128, 128)),
        in_specs=[VMEM] * 7,
        out_specs=(HBM,) * 4,
        scratch_shapes=[pltpu.VMEM((ROWS, WIDTH), f32)] * 3
        + [pltpu.VMEM((128, 128), f32), pltpu.SemaphoreType.DMA((13,))],
        compiler_params=room(8),
        name="finish",
    )(home.reshape(TOK * 16, 128), query, key, value, grad, *terms)
    filter_grad = fg.reshape(64, 2, 128).transpose(1, 0, 2).reshape(2, 8192)
    return (qg[None], kg[None], vg[None], filter_grad)


def solution(mesh):
    tokens = P("seq", "tok", None)
    taps = P("tok", "seq")
    return jax.shard_map(
        body,
        mesh=mesh,
        in_specs=(tokens, tokens, tokens, tokens, taps),
        out_specs=(tokens, tokens, tokens, taps),
        check_vma=False,
    )
```

```python
import jax
import jax.numpy as jnp
import numpy as np
from jax import lax
from jax.experimental import pallas as pl
from jax.experimental.pallas import tpu as pltpu
from jax.sharding import PartitionSpec as P

TOK = 64
SEQ = 4
FIRST_OUT = 42
FIRST_HOME = 42
ROWS = 512
WIDTH = 128
LENGTH = TOK * ROWS
OUTER = 128
INNER = 256
HALF = INNER // 2
CHUNK = 16
SCALE = LENGTH**-0.5 / LENGTH

PIECE = (0, 2, 1, 3)

f32 = jnp.float32
bf16 = jnp.bfloat16
VMEM = pl.BlockSpec(memory_space=pltpu.VMEM)
HBM = pl.BlockSpec(memory_space=pltpu.HBM)
SMEM = pl.BlockSpec(memory_space=pltpu.SMEM)


def split_np(table):
    table = table.astype(np.float32)
    high = table.astype(jnp.bfloat16)
    low = (table - high.astype(np.float32)).astype(jnp.bfloat16)
    return high, low


def order(first):
    devices = list(range(TOK))
    devices[0], devices[first] = first, 0
    return devices


def swap_rows(ref, first, second, size):
    if first == second:
        return
    a, b = ref[pl.ds(first, size), :], ref[pl.ds(second, size), :]
    ref[pl.ds(first, size), :] = b
    ref[pl.ds(second, size), :] = a


def stack_np(real, imag, left):
    high, low = split_np(np.block([[real, imag], [-imag, real]]))
    return np.concatenate([high, high, low], axis=1 if left else 0)


def tables():
    k1 = np.arange(OUTER, dtype=np.float64)[:, None] + 0.25

    def outer_table(first):
        block = np.array(order(first))
        j = np.concatenate([2 * block, 2 * block + 1]).astype(np.float64)[None, :]
        outer = 2.0 * np.pi * np.mod(k1 * j, OUTER) / OUTER
        w = np.stack([np.cos(outer), -np.sin(outer)]).reshape(2, OUTER // CHUNK, CHUNK, OUTER)
        return w.transpose(1, 0, 2, 3).reshape(2 * OUTER, OUTER)

    wh, wl = split_np(outer_table(FIRST_OUT))
    w_fwd = np.concatenate([wh, wh, wl], axis=1)
    vh, vl = split_np(outer_table(FIRST_HOME).T * SCALE)
    w_inv = np.concatenate([vh, vh, vl], axis=1)
    r = np.arange(INNER, dtype=np.float64)[None, :]
    twist = 2.0 * np.pi * k1 * r / LENGTH
    tw = np.stack([np.cos(twist), -np.sin(twist)]).astype(np.float32)
    l = np.arange(HALF, dtype=np.float64)[:, None]
    m = np.arange(HALF, dtype=np.float64)[None, :]
    even = 2.0 * np.pi * np.mod(l * 2 * m, INNER) / INNER
    odd = 2.0 * np.pi * np.mod(l * (2 * m + 1), INNER) / INNER
    t_even = stack_np(np.cos(even), -np.sin(even), False)
    t_odd = stack_np(np.cos(odd), -np.sin(odd), False)
    t_back = stack_np(np.cos(odd.T), -np.sin(odd.T), False)
    return w_fwd, w_inv, tw, t_even, t_odd, t_back


def split(value):
    high = value.astype(bf16)
    low = (value - high.astype(f32)).astype(bf16)
    return high, low


def send_kernel(query_hbm, key_hbm, value_hbm, grad_hbm, out_hbm, query, key, value, grad, tiles, sem, out_sem):
    pairs = ((query_hbm, query), (key_hbm, key), (value_hbm, value), (grad_hbm, grad))
    copies, sends = [], []
    for q in range(4):
        rows = pl.ds(q * 128, 128)
        copies.append([pltpu.make_async_copy(a.at[rows], b.at[rows], sem.at[q, i]) for i, (a, b) in enumerate(pairs)])
        for copy in copies[q]:
            copy.start()
    for q in range(4):
        rows = pl.ds(q * 128, 128)
        for copy in copies[q]:
            copy.wait()
        tiles[q] = (key[rows, :] * value[rows, :]).T
        tiles[4 + q] = (grad[rows, :] * query[rows, :]).T
        for i in (q, 4 + q):
            swap_rows(tiles.at[i], 0, 2 * FIRST_OUT, 2)
            sends.append(pltpu.make_async_copy(tiles.at[i], out_hbm.at[:, i, :], out_sem.at[i]))
            sends[-1].start()
    for send in sends:
        send.wait()


def store_cat(cat, first, left, right):
    lh, ll = split(left)
    rh, rl = split(right)
    rows = pl.ds(first, left.shape[0])
    cat[rows, 0:128] = lh
    cat[rows, 128:256] = rh
    cat[rows, 256:384] = ll
    cat[rows, 384:512] = rl
    cat[rows, 512:640] = lh
    cat[rows, 640:768] = rh


def forward_outer(x, row, wf_ref, tw_ref, cat_e, cat_o):
    xh, xl = split(x)
    a = jnp.dot(wf_ref[...], jnp.concatenate([xh, xl, xh], axis=0), preferred_element_type=f32)
    for i in range(0, OUTER, CHUNK):
        ar, ai = a[2 * i : 2 * i + CHUNK], a[2 * i + CHUNK : 2 * i + 2 * CHUNK]
        tr, ti = tw_ref[0, i : i + CHUNK, :], tw_ref[1, i : i + CHUNK, :]
        br, bi = ar * tr - ai * ti, ar * ti + ai * tr
        first = row * OUTER + i
        store_cat(cat_e, first, br[:, :HALF] + br[:, HALF:], bi[:, :HALF] + bi[:, HALF:])
        store_cat(cat_o, first, br[:, :HALF] - br[:, HALF:], bi[:, :HALF] - bi[:, HALF:])


def inverse_outer(spec_e, spec_o, row, wi_ref, tw_ref, cat):
    for i in range(0, OUTER, CHUNK):
        rows = pl.ds(row * OUTER + i, CHUNK)
        ei, er = spec_e[rows, 0:HALF], spec_e[rows, HALF : 2 * HALF]
        oi, orr = spec_o[rows, 0:HALF], spec_o[rows, HALF : 2 * HALF]
        dr = jnp.concatenate([er + orr, er - orr], axis=1)
        di = jnp.concatenate([ei + oi, ei - oi], axis=1)
        tr, ti = tw_ref[0, i : i + CHUNK, :], tw_ref[1, i : i + CHUNK, :]
        for first, e in ((2 * i, dr * tr + di * ti), (2 * i + CHUNK, di * tr - dr * ti)):
            eh, el = split(e)
            cat[pl.ds(first, CHUNK), :] = eh
            cat[pl.ds(256 + first, CHUNK), :] = el
            cat[pl.ds(512 + first, CHUNK), :] = eh
    return matmul(wi_ref, cat)


def matmul(cat, table):
    return jnp.dot(cat[...], table[...], preferred_element_type=f32)


def taps_kernel(
    part_ref, near_ref, far_ref, wf_ref, tw_ref, te_ref, to_ref, out_hbm, taps, cat_e, cat_o, spec, sem
):
    for k in range(SEQ):
        f_ref, first = (near_ref if k < 2 else far_ref), (k % 2) * 128
        base = part_ref[PIECE[k]] * 16
        for c in range(2):
            for q2 in range(2):
                for h in range(2):
                    taps[c, pl.ds(pl.multiple_of(q2 * 64 + base, 16), 16), pl.ds(h * 128, 128)] = f_ref[
                        pl.ds(first + 4 * q2 + 2 * h + c, 16, stride=8), :
                    ]
    for c in range(2):
        for q2 in range(2):
            swap_rows(taps.at[c], 64 * q2, 64 * q2 + FIRST_OUT, 1)
        forward_outer(taps[c], c, wf_ref, tw_ref, cat_e, cat_o)
    copies = []
    for p, (cat, t_ref) in enumerate(((cat_e, te_ref), (cat_o, to_ref))):
        spec[p] = matmul(cat, t_ref)
        copies.append(pltpu.make_async_copy(spec.at[p], out_hbm.at[p], sem.at[p]))
        copies[p].start()
    for copy in copies:
        copy.wait()


def spectral_kernel(
    recv_ref, taps_ref, wf_ref, wi_ref, tw_ref, te_ref, to_ref, tb_ref,
    out_hbm, cross_hbm,
    cat_e, cat_o, spec_e, spec_o, back, cross, tiles, sem, out_sem,
):
    sends = []
    for c in range(2):
        for sig in range(2):
            x = jnp.concatenate(
                [
                    jnp.concatenate(
                        [recv_ref[pl.ds(c * 8 + sig * 4 + 2 * q2 + h, 64, stride=16), :] for h in range(2)],
                        axis=1,
                    )
                    for q2 in range(2)
                ],
                axis=0,
            )
            forward_outer(x, 2 * c + sig, wf_ref, tw_ref, cat_e, cat_o)

    def product(p, cat, spec):
        for c in range(2):
            for i in range(0, OUTER, CHUNK):
                g, k = pl.ds(2 * c * OUTER + i, CHUNK), pl.ds((2 * c + 1) * OUTER + i, CHUNK)
                h = pl.ds(c * OUTER + i, CHUNK)
                gr, gi = spec[g, 0:HALF], spec[g, HALF : 2 * HALF]
                cr, ci = spec[k, 0:HALF], spec[k, HALF : 2 * HALF]
                hr, hi = taps_ref[p, h, 0:HALF], taps_ref[p, h, HALF : 2 * HALF]
                store_cat(cat, 2 * c * OUTER + i, gr * hi + gi * hr, gr * hr - gi * hi)
                store_cat(cat, (2 * c + 1) * OUTER + i, hr * ci - hi * cr, hr * cr + hi * ci)
                cross[p, h, 0:HALF] = gr * ci - gi * cr
                cross[p, h, HALF : 2 * HALF] = gr * cr + gi * ci

    spec_e[...] = matmul(cat_e, te_ref)
    spec_o[...] = matmul(cat_o, to_ref)
    product(0, cat_e, spec_e)
    spec_e[...] = matmul(cat_e, te_ref)
    product(1, cat_o, spec_o)
    sends.append(pltpu.make_async_copy(cross, cross_hbm, sem))
    sends[0].start()
    spec_o[...] = matmul(cat_o, tb_ref)

    for c in range(2):
        for sig in range(2):
            y = inverse_outer(spec_e, spec_o, 2 * c + sig, wi_ref, tw_ref, back.at[2 * c + sig])
            for q2 in range(2):
                for h in range(2):
                    i = c * 8 + sig * 4 + 2 * q2 + h
                    tiles[i] = y[q2 * 64 : q2 * 64 + 64, h * 128 : h * 128 + 128]
                    sends.append(pltpu.make_async_copy(tiles.at[i], out_hbm.at[:, i, :], out_sem.at[i]))
                    sends[-1].start()
    for send in sends:
        send.wait()


def terms_kernel(
    part_ref, cross_ref, wi_ref, tw_ref, te_ref, tb_ref, own_ref, give_ref, cat_e, cat_o, spec_e, spec_o, back, terms
):
    for p, cat in enumerate((cat_e, cat_o)):
        for c in range(2):
            rows = pl.ds(c * OUTER, OUTER)
            store_cat(cat, c * OUTER, cross_ref[p, rows, 0:HALF], cross_ref[p, rows, HALF : 2 * HALF])
    spec_e[...] = matmul(cat_e, te_ref)
    spec_o[...] = matmul(cat_o, tb_ref)
    for c in range(2):
        y = inverse_outer(spec_e, spec_o, c, wi_ref, tw_ref, back.at[c])
        for q2 in range(2):
            for h in range(2):
                terms[pl.ds(4 * q2 + 2 * h + c, 64, stride=8), :] = y[
                    q2 * 64 : q2 * 64 + 64, h * 128 : h * 128 + 128
                ]
    swap_rows(terms, 0, 8 * FIRST_HOME, 8)
    for k in range(SEQ):
        ref, first = (own_ref if k < 2 else give_ref), (k % 2) * 128
        ref[first : first + 128, :] = terms[
            pl.ds(pl.multiple_of(part_ref[PIECE[k]] * 128, 128), 128), :
        ]


def finish_kernel(
    recv_ref, query_ref, key_ref, value_ref, grad_ref, own_ref, far_ref,
    qg_hbm, kg_hbm, vg_hbm, fg_hbm,
    qg, kg, vg, fg, tiles, sem,
):
    fg[...] = own_ref[...] + far_ref[...]
    copies = [pltpu.make_async_copy(fg, fg_hbm, sem.at[12])]
    copies[0].start()
    for q in range(4):
        rows = pl.ds(q * 128, 128)
        for i in (q, 4 + q):
            tiles[i] = recv_ref[pl.ds(i, 128, stride=8), :]
            swap_rows(tiles.at[i], 0, 2 * FIRST_HOME, 2)
        conv, ggrad = tiles[q].T, tiles[4 + q].T
        qg[rows, :] = grad_ref[rows, :] * conv
        kg[rows, :] = ggrad * value_ref[rows, :]
        vg[rows, :] = ggrad * key_ref[rows, :]
        for i, (a, b) in enumerate(((qg, qg_hbm), (kg, kg_hbm), (vg, vg_hbm))):
            copy = pltpu.make_async_copy(a.at[rows], b.at[rows], sem.at[3 * q + i])
            copy.start()
            copies.append(copy)
    for copy in copies:
        copy.wait()


def shape(*dims, kind=f32):
    return jax.ShapeDtypeStruct(dims, kind)


def room(mib):
    return pltpu.CompilerParams(vmem_limit_bytes=mib * 2**20)


def cost(units):
    return pl.CostEstimate(flops=units * 800_000_000, bytes_accessed=units * 1_000_000, transcendentals=0)


def body(query_gate, key_gate, value_input, out_grad, filter_param):
    query, key, value, grad = (a.reshape(ROWS, WIDTH) for a in (query_gate, key_gate, value_input, out_grad))
    me = lax.axis_index("seq")
    parts = jnp.bitwise_xor(me, jnp.arange(SEQ, dtype=jnp.int32)).astype(jnp.int32)

    def swap(block, k):
        return lax.ppermute(block, "seq", [(s, s ^ k) for s in range(SEQ)])

    def exchange(block, first):
        return lax.all_to_all(
            block.reshape(TOK, 16, 128),
            "tok",
            split_axis=0,
            concat_axis=0,
            tiled=True,
            axis_index_groups=[order(first)],
        )

    own = filter_param.reshape(2, 64, 128).transpose(1, 0, 2).reshape(128, 128)
    near = jnp.concatenate([own, swap(own, 2)], axis=0)
    far = swap(near, 1)
    w_fwd, w_inv, tw, t_even, t_odd, t_back = tables()
    sent = pl.pallas_call(
        send_kernel,
        out_shape=shape(TOK * 2, 8, 128),
        in_specs=[HBM] * 4,
        out_specs=HBM,
        scratch_shapes=[pltpu.VMEM((ROWS, WIDTH), f32)] * 4
        + [pltpu.VMEM((8, 128, 128), f32), pltpu.SemaphoreType.DMA((4, 4)), pltpu.SemaphoreType.DMA((8,))],
        compiler_params=room(60),
        name="send",
    )(query, key, value, grad)
    recv = exchange(sent, FIRST_OUT)
    taps = pl.pallas_call(
        taps_kernel,
        out_shape=shape(2, 2 * OUTER, INNER),
        in_specs=[SMEM] + [VMEM] * 6,
        out_specs=HBM,
        scratch_shapes=[pltpu.VMEM((2, OUTER, INNER), f32)]
        + [pltpu.VMEM((2 * OUTER, 3 * INNER), bf16)] * 2
        + [pltpu.VMEM((2, 2 * OUTER, INNER), f32), pltpu.SemaphoreType.DMA((2,))],
        compiler_params=room(8),
        cost_estimate=cost(1),
        name="taps",
    )(parts, near, far, w_fwd, tw, t_even, t_odd)
    back, cross = pl.pallas_call(
        spectral_kernel,
        out_shape=(shape(TOK, 16, 128), pltpu.HBM((2, 2 * OUTER, INNER), f32)),
        in_specs=[VMEM] * 8,
        out_specs=(HBM, HBM),
        scratch_shapes=[pltpu.VMEM((4 * OUTER, 3 * INNER), bf16)] * 2
        + [pltpu.VMEM((4 * OUTER, INNER), f32)] * 2
        + [pltpu.VMEM((4, 6 * OUTER, INNER), bf16), pltpu.VMEM((2, 2 * OUTER, INNER), f32)]
        + [pltpu.VMEM((16, TOK, 128), f32), pltpu.SemaphoreType.DMA, pltpu.SemaphoreType.DMA((16,))],
        compiler_params=room(8),
        cost_estimate=cost(4),
        name="spectral",
    )(recv.reshape(TOK * 16, 128), taps, w_fwd, w_inv, tw, t_even, t_odd, t_back)
    home = exchange(back, FIRST_HOME)
    kept, given = pl.pallas_call(
        terms_kernel,
        out_shape=(shape(256, 128),) * 2,
        in_specs=[SMEM] + [VMEM] * 5,
        out_specs=(VMEM,) * 2,
        scratch_shapes=[pltpu.VMEM((2 * OUTER, 3 * INNER), bf16)] * 2
        + [pltpu.VMEM((2 * OUTER, INNER), f32)] * 2
        + [pltpu.VMEM((2, 6 * OUTER, INNER), bf16), pltpu.VMEM((SEQ * 128, 128), f32)],
        compiler_params=room(8),
        cost_estimate=cost(1),
        name="terms",
    )(parts, cross, w_inv, tw, t_even, t_back)
    paired = kept + swap(given, 1)
    terms = (paired[:128], swap(paired[128:], 2))
    qg, kg, vg, fg = pl.pallas_call(
        finish_kernel,
        out_shape=(*[shape(ROWS, WIDTH)] * 3, shape(128, 128)),
        in_specs=[VMEM] * 7,
        out_specs=(HBM,) * 4,
        scratch_shapes=[pltpu.VMEM((ROWS, WIDTH), f32)] * 3
        + [pltpu.VMEM((128, 128), f32), pltpu.VMEM((8, 128, 128), f32), pltpu.SemaphoreType.DMA((13,))],
        compiler_params=room(8),
        name="finish",
    )(home.reshape(TOK * 16, 128), query, key, value, grad, *terms)
    filter_grad = fg.reshape(64, 2, 128).transpose(1, 0, 2).reshape(2, 8192)
    return (qg[None], kg[None], vg[None], filter_grad)


def solution(mesh):
    tokens = P("seq", "tok", None)
    taps = P("tok", "seq")
    return jax.shard_map(
        body,
        mesh=mesh,
        in_specs=(tokens, tokens, tokens, tokens, taps),
        out_specs=(tokens, tokens, tokens, taps),
        check_vma=False,
    )
```

```python
import jax
import jax.numpy as jnp
import numpy as np
from jax import lax
from jax.experimental import pallas as pl
from jax.experimental.pallas import tpu as pltpu
from jax.sharding import PartitionSpec as P

TOK = 64
SEQ = 4
FIRST_OUT = 42
FIRST_HOME = 40
ROWS = 512
WIDTH = 128
LENGTH = TOK * ROWS
OUTER = 128
INNER = 256
HALF = INNER // 2
CHUNK = 16
SCALE = LENGTH**-0.5 / LENGTH

PIECE = (0, 2, 1, 3)

f32 = jnp.float32
bf16 = jnp.bfloat16
VMEM = pl.BlockSpec(memory_space=pltpu.VMEM)
HBM = pl.BlockSpec(memory_space=pltpu.HBM)
SMEM = pl.BlockSpec(memory_space=pltpu.SMEM)


def split_np(table):
    table = table.astype(np.float32)
    high = table.astype(jnp.bfloat16)
    low = (table - high.astype(np.float32)).astype(jnp.bfloat16)
    return high, low


def order(first):
    devices = list(range(TOK))
    devices[0], devices[first] = first, 0
    return devices


def swap_rows(ref, first, second, size):
    if first == second:
        return
    a, b = ref[pl.ds(first, size), :], ref[pl.ds(second, size), :]
    ref[pl.ds(first, size), :] = b
    ref[pl.ds(second, size), :] = a


def stack_np(real, imag, left):
    high, low = split_np(np.block([[real, imag], [-imag, real]]))
    return np.concatenate([high, high, low], axis=1 if left else 0)


def tables():
    k1 = np.arange(OUTER, dtype=np.float64)[:, None] + 0.25

    def outer_table(first):
        block = np.array(order(first))
        j = np.concatenate([2 * block, 2 * block + 1]).astype(np.float64)[None, :]
        outer = 2.0 * np.pi * np.mod(k1 * j, OUTER) / OUTER
        w = np.stack([np.cos(outer), -np.sin(outer)]).reshape(2, OUTER // CHUNK, CHUNK, OUTER)
        return w.transpose(1, 0, 2, 3).reshape(2 * OUTER, OUTER)

    wh, wl = split_np(outer_table(FIRST_OUT))
    w_fwd = np.concatenate([wh, wh, wl], axis=1)
    vh, vl = split_np(outer_table(FIRST_HOME).T * SCALE)
    w_inv = np.concatenate([vh, vh, vl], axis=1)
    r = np.arange(INNER, dtype=np.float64)[None, :]
    twist = 2.0 * np.pi * k1 * r / LENGTH
    tw = np.stack([np.cos(twist), -np.sin(twist)]).astype(np.float32)
    l = np.arange(HALF, dtype=np.float64)[:, None]
    m = np.arange(HALF, dtype=np.float64)[None, :]
    even = 2.0 * np.pi * np.mod(l * 2 * m, INNER) / INNER
    odd = 2.0 * np.pi * np.mod(l * (2 * m + 1), INNER) / INNER
    t_even = stack_np(np.cos(even), -np.sin(even), False)
    t_odd = stack_np(np.cos(odd), -np.sin(odd), False)
    t_back = stack_np(np.cos(odd.T), -np.sin(odd.T), False)
    return w_fwd, w_inv, tw, t_even, t_odd, t_back


def split(value):
    high = value.astype(bf16)
    low = (value - high.astype(f32)).astype(bf16)
    return high, low


def send_kernel(query_hbm, key_hbm, value_hbm, grad_hbm, out_hbm, query, key, value, grad, tiles, sem, out_sem):
    pairs = ((query_hbm, query), (key_hbm, key), (value_hbm, value), (grad_hbm, grad))
    copies, sends = [], []
    for q in range(4):
        rows = pl.ds(q * 128, 128)
        copies.append([pltpu.make_async_copy(a.at[rows], b.at[rows], sem.at[q, i]) for i, (a, b) in enumerate(pairs)])
        for copy in copies[q]:
            copy.start()
    for q in range(4):
        rows = pl.ds(q * 128, 128)
        for copy in copies[q]:
            copy.wait()
        tiles[q] = (key[rows, :] * value[rows, :]).T
        tiles[4 + q] = (grad[rows, :] * query[rows, :]).T
        for i in (q, 4 + q):
            swap_rows(tiles.at[i], 0, 2 * FIRST_OUT, 2)
            sends.append(pltpu.make_async_copy(tiles.at[i], out_hbm.at[:, i, :], out_sem.at[i]))
            sends[-1].start()
    for send in sends:
        send.wait()


def store_cat(cat, first, left, right):
    lh, ll = split(left)
    rh, rl = split(right)
    rows = pl.ds(first, left.shape[0])
    cat[rows, 0:128] = lh
    cat[rows, 128:256] = rh
    cat[rows, 256:384] = ll
    cat[rows, 384:512] = rl
    cat[rows, 512:640] = lh
    cat[rows, 640:768] = rh


def forward_outer(x, row, wf_ref, tw_ref, cat_e, cat_o):
    xh, xl = split(x)
    a = jnp.dot(wf_ref[...], jnp.concatenate([xh, xl, xh], axis=0), preferred_element_type=f32)
    for i in range(0, OUTER, CHUNK):
        ar, ai = a[2 * i : 2 * i + CHUNK], a[2 * i + CHUNK : 2 * i + 2 * CHUNK]
        tr, ti = tw_ref[0, i : i + CHUNK, :], tw_ref[1, i : i + CHUNK, :]
        br, bi = ar * tr - ai * ti, ar * ti + ai * tr
        first = row * OUTER + i
        store_cat(cat_e, first, br[:, :HALF] + br[:, HALF:], bi[:, :HALF] + bi[:, HALF:])
        store_cat(cat_o, first, br[:, :HALF] - br[:, HALF:], bi[:, :HALF] - bi[:, HALF:])


def inverse_outer(spec_e, spec_o, row, wi_ref, tw_ref, cat):
    for i in range(0, OUTER, CHUNK):
        rows = pl.ds(row * OUTER + i, CHUNK)
        ei, er = spec_e[rows, 0:HALF], spec_e[rows, HALF : 2 * HALF]
        oi, orr = spec_o[rows, 0:HALF], spec_o[rows, HALF : 2 * HALF]
        dr = jnp.concatenate([er + orr, er - orr], axis=1)
        di = jnp.concatenate([ei + oi, ei - oi], axis=1)
        tr, ti = tw_ref[0, i : i + CHUNK, :], tw_ref[1, i : i + CHUNK, :]
        for first, e in ((2 * i, dr * tr + di * ti), (2 * i + CHUNK, di * tr - dr * ti)):
            eh, el = split(e)
            cat[pl.ds(first, CHUNK), :] = eh
            cat[pl.ds(256 + first, CHUNK), :] = el
            cat[pl.ds(512 + first, CHUNK), :] = eh
    return matmul(wi_ref, cat)


def matmul(cat, table):
    return jnp.dot(cat[...], table[...], preferred_element_type=f32)


def taps_kernel(
    part_ref, near_ref, far_ref, wf_ref, tw_ref, te_ref, to_ref, out_hbm, taps, cat_e, cat_o, spec, sem
):
    for k in range(SEQ):
        f_ref, first = (near_ref if k < 2 else far_ref), (k % 2) * 128
        base = part_ref[PIECE[k]] * 16
        for c in range(2):
            for q2 in range(2):
                for h in range(2):
                    taps[c, pl.ds(pl.multiple_of(q2 * 64 + base, 16), 16), pl.ds(h * 128, 128)] = f_ref[
                        pl.ds(first + 4 * q2 + 2 * h + c, 16, stride=8), :
                    ]
    for c in range(2):
        for q2 in range(2):
            swap_rows(taps.at[c], 64 * q2, 64 * q2 + FIRST_OUT, 1)
        forward_outer(taps[c], c, wf_ref, tw_ref, cat_e, cat_o)
    copies = []
    for p, (cat, t_ref) in enumerate(((cat_e, te_ref), (cat_o, to_ref))):
        spec[p] = matmul(cat, t_ref)
        copies.append(pltpu.make_async_copy(spec.at[p], out_hbm.at[p], sem.at[p]))
        copies[p].start()
    for copy in copies:
        copy.wait()


def spectral_kernel(
    recv_ref, taps_ref, wf_ref, wi_ref, tw_ref, te_ref, to_ref, tb_ref,
    out_hbm, cross_hbm,
    cat_e, cat_o, spec_e, spec_o, back, cross, tiles, sem, out_sem,
):
    sends = []
    for c in range(2):
        for sig in range(2):
            x = jnp.concatenate(
                [
                    jnp.concatenate(
                        [recv_ref[pl.ds(c * 8 + sig * 4 + 2 * q2 + h, 64, stride=16), :] for h in range(2)],
                        axis=1,
                    )
                    for q2 in range(2)
                ],
                axis=0,
            )
            forward_outer(x, 2 * c + sig, wf_ref, tw_ref, cat_e, cat_o)

    def product(p, cat, spec):
        for c in range(2):
            for i in range(0, OUTER, CHUNK):
                g, k = pl.ds(2 * c * OUTER + i, CHUNK), pl.ds((2 * c + 1) * OUTER + i, CHUNK)
                h = pl.ds(c * OUTER + i, CHUNK)
                gr, gi = spec[g, 0:HALF], spec[g, HALF : 2 * HALF]
                cr, ci = spec[k, 0:HALF], spec[k, HALF : 2 * HALF]
                hr, hi = taps_ref[p, h, 0:HALF], taps_ref[p, h, HALF : 2 * HALF]
                store_cat(cat, 2 * c * OUTER + i, gr * hi + gi * hr, gr * hr - gi * hi)
                store_cat(cat, (2 * c + 1) * OUTER + i, hr * ci - hi * cr, hr * cr + hi * ci)
                cross[p, h, 0:HALF] = gr * ci - gi * cr
                cross[p, h, HALF : 2 * HALF] = gr * cr + gi * ci

    spec_e[...] = matmul(cat_e, te_ref)
    spec_o[...] = matmul(cat_o, to_ref)
    product(0, cat_e, spec_e)
    spec_e[...] = matmul(cat_e, te_ref)
    product(1, cat_o, spec_o)
    sends.append(pltpu.make_async_copy(cross, cross_hbm, sem))
    sends[0].start()
    spec_o[...] = matmul(cat_o, tb_ref)

    for c in range(2):
        for sig in range(2):
            y = inverse_outer(spec_e, spec_o, 2 * c + sig, wi_ref, tw_ref, back.at[2 * c + sig])
            for q2 in range(2):
                for h in range(2):
                    i = c * 8 + sig * 4 + 2 * q2 + h
                    tiles[i] = y[q2 * 64 : q2 * 64 + 64, h * 128 : h * 128 + 128]
                    sends.append(pltpu.make_async_copy(tiles.at[i], out_hbm.at[:, i, :], out_sem.at[i]))
                    sends[-1].start()
    for send in sends:
        send.wait()


def terms_kernel(
    part_ref, cross_ref, wi_ref, tw_ref, te_ref, tb_ref, own_ref, give_ref, cat_e, cat_o, spec_e, spec_o, back, terms
):
    for p, cat in enumerate((cat_e, cat_o)):
        for c in range(2):
            rows = pl.ds(c * OUTER, OUTER)
            store_cat(cat, c * OUTER, cross_ref[p, rows, 0:HALF], cross_ref[p, rows, HALF : 2 * HALF])
    spec_e[...] = matmul(cat_e, te_ref)
    spec_o[...] = matmul(cat_o, tb_ref)
    for c in range(2):
        y = inverse_outer(spec_e, spec_o, c, wi_ref, tw_ref, back.at[c])
        for q2 in range(2):
            for h in range(2):
                terms[pl.ds(4 * q2 + 2 * h + c, 64, stride=8), :] = y[
                    q2 * 64 : q2 * 64 + 64, h * 128 : h * 128 + 128
                ]
    swap_rows(terms, 0, 8 * FIRST_HOME, 8)
    for k in range(SEQ):
        ref, first = (own_ref if k < 2 else give_ref), (k % 2) * 128
        ref[first : first + 128, :] = terms[
            pl.ds(pl.multiple_of(part_ref[PIECE[k]] * 128, 128), 128), :
        ]


def finish_kernel(
    recv_ref, query_ref, key_ref, value_ref, grad_ref, own_ref, far_ref,
    qg_hbm, kg_hbm, vg_hbm, fg_hbm,
    qg, kg, vg, fg, tiles, sem,
):
    fg[...] = own_ref[...] + far_ref[...]
    copies = [pltpu.make_async_copy(fg, fg_hbm, sem.at[12])]
    copies[0].start()
    for q in range(4):
        rows = pl.ds(q * 128, 128)
        for i in (q, 4 + q):
            tiles[i] = recv_ref[pl.ds(i, 128, stride=8), :]
            swap_rows(tiles.at[i], 0, 2 * FIRST_HOME, 2)
        conv, ggrad = tiles[q].T, tiles[4 + q].T
        qg[rows, :] = grad_ref[rows, :] * conv
        kg[rows, :] = ggrad * value_ref[rows, :]
        vg[rows, :] = ggrad * key_ref[rows, :]
        for i, (a, b) in enumerate(((qg, qg_hbm), (kg, kg_hbm), (vg, vg_hbm))):
            copy = pltpu.make_async_copy(a.at[rows], b.at[rows], sem.at[3 * q + i])
            copy.start()
            copies.append(copy)
    for copy in copies:
        copy.wait()


def shape(*dims, kind=f32):
    return jax.ShapeDtypeStruct(dims, kind)


def room(mib):
    return pltpu.CompilerParams(vmem_limit_bytes=mib * 2**20)


def cost(units):
    return pl.CostEstimate(flops=units * 800_000_000, bytes_accessed=units * 1_000_000, transcendentals=0)


def body(query_gate, key_gate, value_input, out_grad, filter_param):
    query, key, value, grad = (a.reshape(ROWS, WIDTH) for a in (query_gate, key_gate, value_input, out_grad))
    me = lax.axis_index("seq")
    parts = jnp.bitwise_xor(me, jnp.arange(SEQ, dtype=jnp.int32)).astype(jnp.int32)

    def swap(block, k):
        return lax.ppermute(block, "seq", [(s, s ^ k) for s in range(SEQ)])

    def exchange(block, first):
        return lax.all_to_all(
            block.reshape(TOK, 16, 128),
            "tok",
            split_axis=0,
            concat_axis=0,
            tiled=True,
            axis_index_groups=[order(first)],
        )

    own = filter_param.reshape(2, 64, 128).transpose(1, 0, 2).reshape(128, 128)
    near = jnp.concatenate([own, swap(own, 2)], axis=0)
    far = swap(near, 1)
    w_fwd, w_inv, tw, t_even, t_odd, t_back = tables()
    sent = pl.pallas_call(
        send_kernel,
        out_shape=shape(TOK * 2, 8, 128),
        in_specs=[HBM] * 4,
        out_specs=HBM,
        scratch_shapes=[pltpu.VMEM((ROWS, WIDTH), f32)] * 4
        + [pltpu.VMEM((8, 128, 128), f32), pltpu.SemaphoreType.DMA((4, 4)), pltpu.SemaphoreType.DMA((8,))],
        compiler_params=room(60),
        name="send",
    )(query, key, value, grad)
    recv = exchange(sent, FIRST_OUT)
    taps = pl.pallas_call(
        taps_kernel,
        out_shape=shape(2, 2 * OUTER, INNER),
        in_specs=[SMEM] + [VMEM] * 6,
        out_specs=HBM,
        scratch_shapes=[pltpu.VMEM((2, OUTER, INNER), f32)]
        + [pltpu.VMEM((2 * OUTER, 3 * INNER), bf16)] * 2
        + [pltpu.VMEM((2, 2 * OUTER, INNER), f32), pltpu.SemaphoreType.DMA((2,))],
        compiler_params=room(8),
        cost_estimate=cost(1),
        name="taps",
    )(parts, near, far, w_fwd, tw, t_even, t_odd)
    back, cross = pl.pallas_call(
        spectral_kernel,
        out_shape=(shape(TOK, 16, 128), pltpu.HBM((2, 2 * OUTER, INNER), f32)),
        in_specs=[VMEM] * 8,
        out_specs=(HBM, HBM),
        scratch_shapes=[pltpu.VMEM((4 * OUTER, 3 * INNER), bf16)] * 2
        + [pltpu.VMEM((4 * OUTER, INNER), f32)] * 2
        + [pltpu.VMEM((4, 6 * OUTER, INNER), bf16), pltpu.VMEM((2, 2 * OUTER, INNER), f32)]
        + [pltpu.VMEM((16, TOK, 128), f32), pltpu.SemaphoreType.DMA, pltpu.SemaphoreType.DMA((16,))],
        compiler_params=room(8),
        cost_estimate=cost(4),
        name="spectral",
    )(recv.reshape(TOK * 16, 128), taps, w_fwd, w_inv, tw, t_even, t_odd, t_back)
    home = exchange(back, FIRST_HOME)
    kept, given = pl.pallas_call(
        terms_kernel,
        out_shape=(shape(256, 128),) * 2,
        in_specs=[SMEM] + [VMEM] * 5,
        out_specs=(VMEM,) * 2,
        scratch_shapes=[pltpu.VMEM((2 * OUTER, 3 * INNER), bf16)] * 2
        + [pltpu.VMEM((2 * OUTER, INNER), f32)] * 2
        + [pltpu.VMEM((2, 6 * OUTER, INNER), bf16), pltpu.VMEM((SEQ * 128, 128), f32)],
        compiler_params=room(8),
        cost_estimate=cost(1),
        name="terms",
    )(parts, cross, w_inv, tw, t_even, t_back)
    paired = kept + swap(given, 1)
    terms = (paired[:128], swap(paired[128:], 2))
    qg, kg, vg, fg = pl.pallas_call(
        finish_kernel,
        out_shape=(*[shape(ROWS, WIDTH)] * 3, shape(128, 128)),
        in_specs=[VMEM] * 7,
        out_specs=(HBM,) * 4,
        scratch_shapes=[pltpu.VMEM((ROWS, WIDTH), f32)] * 3
        + [pltpu.VMEM((128, 128), f32), pltpu.VMEM((8, 128, 128), f32), pltpu.SemaphoreType.DMA((13,))],
        compiler_params=room(8),
        name="finish",
    )(home.reshape(TOK * 16, 128), query, key, value, grad, *terms)
    filter_grad = fg.reshape(64, 2, 128).transpose(1, 0, 2).reshape(2, 8192)
    return (qg[None], kg[None], vg[None], filter_grad)


def solution(mesh):
    tokens = P("seq", "tok", None)
    taps = P("tok", "seq")
    return jax.shard_map(
        body,
        mesh=mesh,
        in_specs=(tokens, tokens, tokens, tokens, taps),
        out_specs=(tokens, tokens, tokens, taps),
        check_vma=False,
    )
```
